32 devices in a mesh: tile: 8 (over z, x), mode: 4 (over y, core).
Axes of the slice: x: 2, y: 2, z: 4, core: 2. Of those that a mesh axis runs over, the one named last changes fastest.
Arguments:
- object_real: float32 [8, 2, 384, 384], P('tile', None, 'mode'), may hold values from 0.6 to 1.2
- object_imag: float32 [8, 2, 384, 384], P('tile', None, 'mode'), may hold values from -0.4 to 0.4
- probe: float32 [2, 8, 256, 256], P(None, 'mode'), may hold values from -1.5 to 1.5
- measured: float32 [8, 2, 256, 256], P('tile'), may hold values from 0.2 to 1.6
- positions: int32 [8, 2, 2], P('tile'), may hold values from 0 to 128
Outputs:
- object_grad_real: float32 [8, 2, 384, 384], P('tile', None, 'mode')
- object_grad_imag: float32 [8, 2, 384, 384], P('tile', None, 'mode')
- probe_grad: float32 [2, 8, 256, 256], P(None, 'mode')
The draws below stay inside these ranges and needn't reach their ends.
All inputs are finite; a program needn't handle non-finite values.
Results may differ from the reference program's by a relative error of at most 0.0003.
Values sent between devices are 32-bit elements; how exact they have to be, the bound alone decides.
No kernel may reach another device: no remote copies, remote signals or barrier semaphores. Data moves between devices by JAX's collectives and lax.ppermute only.
A program may use at most 128 MiB of HBM per device.

```python
import math
import jax
import jax.numpy as jnp
from jax import lax

PX = 256
TILE_PX = 384
MARGIN = 64
MODES = 8
SLICES = 2
FRAMES = 2
TILES = 8


def place_ends(drawn, key, low, high):
    longest = drawn.shape.index(max(drawn.shape))
    spots = []
    for shift in (0, 1):
        where = [jax.random.randint(jax.random.fold_in(key, axis), (), 0, length) for axis, length in enumerate(drawn.shape)]
        where[longest] = (where[longest] + shift) % drawn.shape[longest]
        spots.append(tuple(where))
    return drawn.at[spots[0]].set(low).at[spots[1]].set(high)


def steps_of(key, dims, split, low, high):
    def one(axis_at, blocks):
        draws = jax.random.uniform(jax.random.fold_in(jax.random.fold_in(key, 6), axis_at), (blocks,), jnp.float32, low / len(split), high / len(split))
        return jnp.repeat(jnp.exp(draws), dims[axis_at] // blocks).reshape((-1,) + (1,) * (len(dims) - axis_at - 1))

    level = one(*split[0])
    for cut in split[1:]:
        level = level * one(*cut)
    return level


def gaussian(key, dims, scale, most, cuts=(), held_as=jnp.bfloat16):
    result = jax.random.normal(key, dims, jnp.float32) * scale
    if len(cuts) > 0:
        result = steps_of(key, dims, cuts, -0.22, 0.18) * result
    return jnp.clip(result, min=-most, max=most).astype(held_as)


def setup_inputs(seed: int = 0) -> dict:
    key_of = jax.random.split(jax.random.key(seed), 6)
    object_real = jnp.clip(0.6 + 0.6 * jax.random.uniform(key_of[0], (TILES, SLICES, TILE_PX, TILE_PX), jnp.float32) ** steps_of(key_of[0], (TILES, SLICES, TILE_PX, TILE_PX), ((0, 8), (2, 4)), -0.2, 0.2), 0.6, 1.2)
    object_imag = jnp.clip(jax.random.uniform(key_of[1], (TILES, SLICES, TILE_PX, TILE_PX), jnp.float32, -0.4, 0.4) * steps_of(key_of[1], (TILES, SLICES, TILE_PX, TILE_PX), ((0, 8), (2, 4)), -0.4, 0.0), -0.4, 0.4)
    probe = gaussian(key_of[2], (2, MODES, PX, PX), 0.25, 1.5, ((1, 4),), jnp.float32)
    measured = jnp.clip(0.2 + 1.4 * jax.random.uniform(key_of[3], (TILES, FRAMES, PX, PX), jnp.float32) ** steps_of(key_of[3], (TILES, FRAMES, PX, PX), ((0, 8),), -0.2, 0.2), 0.2, 1.6)
    positions = place_ends(jax.random.randint(key_of[4], (TILES, FRAMES, 2), 0, TILE_PX - PX + 1), jax.random.fold_in(key_of[4], 1), 0, TILE_PX - PX).astype(jnp.int32)
    return {"object_real": object_real, "object_imag": object_imag, "probe": probe, "measured": measured, "positions": positions}


amplitude_floor = 0.1
fresnel_number = 40.0

def tables(width):
    index = jnp.arange(width, dtype=jnp.int32)
    product = index[:, None] * index[None, :] % width
    angle = product.astype(jnp.float32) * (-2.0 * math.pi / width)
    scaling = 1.0 / math.sqrt(width)
    freq = ((index + width // 2) % width - width // 2).astype(jnp.float32) / width
    phase = -math.pi * fresnel_number * (freq[:, None] ** 2 + freq[None, :] ** 2)
    return (jnp.cos(angle) * scaling, jnp.sin(angle) * scaling, jnp.cos(phase), jnp.sin(phase))

def transform(real_part, imag_part, cos_table, sin_table):
    highest = lax.Precision.HIGHEST
    left_re = jnp.einsum('jk,mkl->mjl', cos_table, real_part, precision=highest) - jnp.einsum('jk,mkl->mjl', sin_table, imag_part, precision=highest)
    left_im = jnp.einsum('jk,mkl->mjl', cos_table, imag_part, precision=highest) + jnp.einsum('jk,mkl->mjl', sin_table, real_part, precision=highest)
    out_re = jnp.einsum('mjk,kl->mjl', left_re, cos_table, precision=highest) - jnp.einsum('mjk,kl->mjl', left_im, sin_table, precision=highest)
    out_im = jnp.einsum('mjk,kl->mjl', left_re, sin_table, precision=highest) + jnp.einsum('mjk,kl->mjl', left_im, cos_table, precision=highest)
    return (out_re, out_im)

def forward(crop_re, crop_im, probe_re, probe_im, cos_table, sin_table, kernel_re, kernel_im):
    wave_re, wave_im = (probe_re, probe_im)
    slices = crop_re.shape[0]
    for layer in range(slices):
        trans_re, trans_im = (crop_re[layer], crop_im[layer])
        wave_re, wave_im = (wave_re * trans_re - wave_im * trans_im, wave_re * trans_im + wave_im * trans_re)
        if layer + 1 < slices:
            spec_re, spec_im = transform(wave_re, wave_im, cos_table, sin_table)
            spec_re, spec_im = (spec_re * kernel_re - spec_im * kernel_im, spec_re * kernel_im + spec_im * kernel_re)
            wave_re, wave_im = transform(spec_re, spec_im, cos_table, -sin_table)
    return transform(wave_re, wave_im, cos_table, sin_table)

def tile_loss(tile_re, tile_im, probe, offsets, amplitudes):
    cos_table, sin_table, kernel_re, kernel_im = tables(PX)
    total = jnp.zeros((), jnp.float32)
    zero_index = jnp.zeros((), jnp.int32)
    for frame in range(FRAMES):
        start = (zero_index, offsets[frame, 0].astype(jnp.int32), offsets[frame, 1].astype(jnp.int32))
        crop_re = lax.dynamic_slice(tile_re, start, (SLICES, PX, PX))
        crop_im = lax.dynamic_slice(tile_im, start, (SLICES, PX, PX))
        far_re, far_im = forward(crop_re, crop_im, probe[0], probe[1], cos_table, sin_table, kernel_re, kernel_im)
        intensity = lax.optimization_barrier(jnp.sum(far_re * far_re + far_im * far_im, axis=0))
        amplitude = jnp.sqrt(intensity + amplitude_floor)
        total = total + jnp.sum((amplitude - amplitudes[frame]) ** 2)
    return total

def combine(grads):
    left_part = jnp.concatenate([jnp.zeros_like(grads[:1, ..., -MARGIN:]), grads[:-1, ..., -MARGIN:]], axis=0)
    right_part = jnp.concatenate([grads[1:, ..., :MARGIN], jnp.zeros_like(grads[:1, ..., :MARGIN])], axis=0)
    return grads.at[..., :MARGIN].add(left_part).at[..., -MARGIN:].add(right_part)

def reference(object_real, object_imag, probe, measured, positions):
    grad_fn = jax.grad(tile_loss, argnums=(0, 1, 2))

    def visit(carried, items):
        tile_re, tile_im, offsets, amplitudes = items
        grad_re, grad_im, grad_probe = grad_fn(tile_re, tile_im, probe, offsets, amplitudes)
        return (carried + grad_probe, (grad_re, grad_im))
    probe_grad, (grad_real, grad_imag) = lax.scan(visit, jnp.zeros_like(probe), (object_real, object_imag, positions, measured))
    return (combine(grad_real), combine(grad_imag), probe_grad)
```

```python
import functools
import math

import jax
import jax.numpy as jnp
import numpy as np
from jax import lax
from jax.experimental import pallas as pl
from jax.experimental.pallas import tpu as pltpu
from jax.sharding import PartitionSpec as P

MARGIN = 64


amplitude_floor = 0.1
fresnel_number = 40.0

VM = pl.BlockSpec(memory_space=pltpu.VMEM)
SM = pl.BlockSpec(memory_space=pltpu.SMEM)
F32 = jnp.float32
BF16 = jnp.bfloat16


def real_form(w):
    return np.block([[w.real, w.imag], [-w.imag, w.real]])


def split_np(stack):
    full = np.stack(stack).astype(np.float32)
    hi = full.astype(BF16)
    lo = (full - hi.astype(np.float32)).astype(BF16)
    return np.stack([hi, lo], axis=1)


def make_tables(width):
    half = width // 2
    k = np.arange(width)
    root = np.exp(-2j * np.pi * (np.outer(k, k) % width) / width) / math.sqrt(width)
    even, odd = root[:half, 0::2], root[:half, 1::2]
    freq = ((k + half) % width - half) / width
    line = np.exp(-1j * np.pi * fresnel_number * freq**2)
    move = root.conj() @ (line[:, None] * root)
    plus = (move[:half, :half] + move[:half, half:]) / 2
    minus = (move[:half, :half] - move[:half, half:]) / 2
    dft = [real_form(even), real_form(odd)]
    prop = [real_form(plus), real_form(minus)]
    dft += [a.T for a in dft]
    prop += [a.T for a in prop]
    return split_np(dft), split_np(prop)


def split(x):
    hi = x.astype(BF16)
    return hi, (x - hi.astype(F32)).astype(BF16)


def mul_right(x, tab):
    hi, lo = split(x)
    lhs = jnp.concatenate([hi, lo, hi], axis=1)
    rhs = jnp.concatenate([tab[0], tab[0], tab[1]], axis=0)
    return jnp.dot(lhs, rhs, preferred_element_type=F32)


def mul_left(x, tab):
    hi, lo = split(x)
    lhs = jnp.concatenate([tab[0], tab[0], tab[1]], axis=1)
    rhs = jnp.concatenate([hi, lo, hi], axis=0)
    return jnp.dot(lhs, rhs, preferred_element_type=F32)


def along(x, axis, tabs, pre, post):
    half = x[0].shape[axis] // 2
    lo = [lax.slice_in_dim(p, 0, half, axis=axis) for p in x]
    up = [lax.slice_in_dim(p, half, 2 * half, axis=axis) for p in x]
    if pre:
        lo, up = [a + b for a, b in zip(lo, up)], [a - b for a, b in zip(lo, up)]
    mul = mul_right if axis == 1 else mul_left
    one = mul(jnp.concatenate(lo, axis=axis), tabs[0])
    two = mul(jnp.concatenate(up, axis=axis), tabs[1])
    if post:
        one, two = one + two, one - two
    return tuple(
        jnp.concatenate(
            [lax.slice_in_dim(q, i * half, (i + 1) * half, axis=axis) for q in (one, two)],
            axis=axis,
        )
        for i in range(2)
    )


def planes(x, right, left, pre, post):
    return along(along(x, 1, right, pre, post), 0, left, pre, post)


def load_tabs(ref, order):
    return [(ref[i, 0], ref[i, 1]) for i in order]


def times(a, b):
    return (a[0] * b[0] - a[1] * b[1], a[0] * b[1] + a[1] * b[0])


def conj_times(a, b):
    return (a[0] * b[0] + a[1] * b[1], a[0] * b[1] - a[1] * b[0])


def crop(pieces, where, tile, out):
    rows = pieces[0].shape[1]
    width = out.shape[1]
    for i, piece in enumerate(pieces):
        start = pl.multiple_of(where[2 + i] * rows, 8)
        for part in range(2):
            tile[part, pl.ds(start, rows), :] = piece[part]
    size = tile.shape[1]
    for part in range(2):
        x = pltpu.roll(tile[part], size - where[0], 0)[:width]
        out[part] = pltpu.roll(x, size - where[1], 1)[:, :width]


def spread(grad, where, tile, keep, send, frames):
    width = grad[0].shape[0]
    size = tile.shape[1]
    rows = keep.shape[2]
    for part in range(2):
        x = jnp.concatenate([grad[part], jnp.zeros((width, size - width), F32)], axis=1)
        x = pltpu.roll(x, where[1], 1)
        x = jnp.concatenate([x, jnp.zeros((size - width, size), F32)], axis=0)
        tile[part] = pltpu.roll(x, where[0], 0)
    for k in range(keep.shape[0]):
        for target, owner in ((keep, where[2 + frames * k]), (send, where[3 + frames * k])):
            start = pl.multiple_of(owner * rows, 8)
            for part in range(2):
                target[k, part] = tile[part, pl.ds(start, rows), :]


def sort_kernel(frame_ref, measured_ref, out_ref):
    width = out_ref.shape[0]
    half = width // 2
    i = lax.broadcasted_iota(jnp.int32, (width, width), 0)
    j = lax.broadcasted_iota(jnp.int32, (width, width), 1)
    pick = (j == jnp.where(i < half, 2 * i, 2 * (i - half) + 1)).astype(F32).astype(BF16)
    kcip = (i == jnp.where(j < half, 2 * j, 2 * (j - half) + 1)).astype(F32).astype(BF16)

    def three(x):
        hi = x.astype(BF16)
        rest = x - hi.astype(F32)
        mid = rest.astype(BF16)
        return [hi, mid, (rest - mid.astype(F32)).astype(BF16)]

    x = measured_ref[0, frame_ref[0]]
    x = jnp.dot(
        jnp.concatenate([pick] * 3, axis=1),
        jnp.concatenate(three(x), axis=0),
        preferred_element_type=F32,
    )
    out_ref[...] = jnp.dot(
        jnp.concatenate(three(x), axis=1),
        jnp.concatenate([kcip] * 3, axis=0),
        preferred_element_type=F32,
    )


def first_kernel(count, where, *refs):
    pieces = refs[:count]
    own, peer, tabs, wave, crop_ref, tile = refs[count:]
    crop(pieces, where, tile, crop_ref)
    obj = (crop_ref[0], crop_ref[1])
    right, left = load_tabs(tabs, (0, 1)), load_tabs(tabs, (2, 3))
    n = own.shape[1]
    for mode in range(2 * n):
        src = own if mode < n else peer
        x = times((src[0, mode % n], src[1, mode % n]), obj)
        wave[mode, 0], wave[mode, 1] = planes(x, right, left, True, True)


def second_kernel(count, where, *refs):
    pieces = refs[:count]
    wave, tabs, far, local, crop_ref, tile = refs[count:]
    crop(pieces, where, tile, crop_ref)
    obj = (crop_ref[0], crop_ref[1])
    right, left = load_tabs(tabs, (0, 1)), load_tabs(tabs, (2, 3))
    for mode in range(wave.shape[0]):
        x = times((wave[mode, 0], wave[mode, 1]), obj)
        re, im = planes(x, right, left, True, False)
        far[mode, 0], far[mode, 1] = re, im
        power = re * re + im * im
        local[...] = power if mode == 0 else local[...] + power


def third_kernel(frames, where, mine, other, measured, far, wave, crop_ref, tabs, back, keep, send, tile, acc):
    intensity = mine[...] + other[...]
    factor = 2.0 * (1.0 - measured[...] / jnp.sqrt(intensity + amplitude_floor))
    mine_obj = (crop_ref[0], crop_ref[1])
    right, left = load_tabs(tabs, (2, 3)), load_tabs(tabs, (0, 1))
    for mode in range(far.shape[0]):
        x = (factor * far[mode, 0], factor * far[mode, 1])
        g = planes(x, right, left, False, True)
        grad = conj_times((wave[mode, 0], wave[mode, 1]), g)
        for part in range(2):
            acc[part] = grad[part] if mode == 0 else acc[part] + grad[part]
        back[mode, 0], back[mode, 1] = conj_times(mine_obj, g)
    spread((acc[0], acc[1]), where, tile, keep, send, frames)


def fourth_kernel(frames, where, back, own, peer, crop_ref, tabs, pkeep, psend, keep, send, tile, acc):
    obj = (crop_ref[0], crop_ref[1])
    right, left = load_tabs(tabs, (2, 3)), load_tabs(tabs, (0, 1))
    n = own.shape[1]
    blocks, rows = pkeep.shape[0], pkeep.shape[3]
    for mode in range(2 * n):
        src, dst = (own, pkeep) if mode < n else (peer, psend)
        g = planes((back[mode, 0], back[mode, 1]), right, left, True, True)
        grad = conj_times((src[0, mode % n], src[1, mode % n]), g)
        for part in range(2):
            acc[part] = grad[part] if mode == 0 else acc[part] + grad[part]
        out = conj_times(obj, g)
        for part in range(2):
            for b in range(blocks):
                dst[b, part, mode % n] = out[part][b * rows : (b + 1) * rows]
    spread((acc[0], acc[1]), where, tile, keep, send, frames)


def call(kernel, outs, scratch, flops, *args):
    shapes = [jax.ShapeDtypeStruct(s, F32) for s in outs]
    moved = 4 * sum(math.prod(s) for s in outs) + 4 * sum(a.size for a in args)
    return pl.pallas_call(
        kernel,
        out_shape=shapes,
        in_specs=[SM] + [VM] * (len(args) - 1),
        out_specs=[VM] * len(shapes),
        scratch_shapes=[pltpu.VMEM(s, F32) for s in scratch],
        cost_estimate=pl.CostEstimate(flops=flops, bytes_accessed=moved, transcendentals=0),
        compiler_params=pltpu.CompilerParams(vmem_limit_bytes=56 * 2**20),
    )(*args)


def body(object_real, object_imag, probe, measured, positions):
    count = lax.axis_size("mode")
    tiles = lax.axis_size("tile")
    frames = measured.shape[1]
    cells = count // frames
    width = probe.shape[2]
    size = object_real.shape[3]
    rows = object_real.shape[2]
    slices = object_real.shape[1]
    modes = probe.shape[1]
    if frames != 2 or cells != 2 or slices != 2 or width % tiles:
        raise ValueError("unsupported split")
    dft_np, prop_np = make_tables(width)
    dft, prop = jnp.asarray(dft_np), jnp.asarray(prop_np)
    me = lax.axis_index("mode")
    frame, cell = me % frames, me // frames
    near = [(i, i ^ 1) for i in range(count)]
    far_away = [(i, i ^ frames) for i in range(count)]
    owners = [me, me ^ 1, me ^ frames, me ^ frames ^ 1]
    place = positions[0, frame].astype(jnp.int32)
    where = jnp.stack([place[0], place[1]] + [o.astype(jnp.int32) for o in owners])

    shards = [jnp.stack([object_real[0, s], object_imag[0, s]]) for s in range(slices)]
    from_y = [lax.ppermute(x, "mode", far_away) for x in shards]
    probe_peer = lax.ppermute(probe, "mode", near)
    from_core = [lax.ppermute(x, "mode", near) for x in shards]
    from_diag = [lax.ppermute(x, "mode", near) for x in from_y]

    unit = 4 * 2 * modes * 3 * 2 * width**3 * 2
    field = (2 * modes, 2, width, width)
    tile_shape = (2, size, size)
    part = (2, width, width)
    share = (cells, 2, rows, size)
    (sorted_measured,) = call(
        sort_kernel, [(width, width)], [], unit // 16, frame.astype(jnp.int32)[None], measured
    )
    pieces = [[shards[s], from_core[s], from_y[s], from_diag[s]] for s in range(slices)]
    wave, crop0 = call(
        functools.partial(first_kernel, count),
        [field, part],
        [tile_shape],
        unit,
        where,
        *pieces[0],
        probe,
        probe_peer,
        prop,
    )
    far, local, crop1 = call(
        functools.partial(second_kernel, count),
        [field, (width, width), part],
        [tile_shape],
        unit,
        where,
        *pieces[1],
        wave,
        dft,
    )
    other = lax.ppermute(local, "mode", far_away)
    back, keep1, send1 = call(
        functools.partial(third_kernel, frames),
        [field, share, share],
        [tile_shape, part],
        unit,
        where,
        local,
        other,
        sorted_measured,
        far,
        wave,
        crop1,
        dft,
    )
    block = (tiles, 2, modes, width // tiles, width)
    got1 = lax.ppermute(send1, "mode", near)
    pkeep, psend, keep0, send0 = call(
        functools.partial(fourth_kernel, frames),
        [block, block, share, share],
        [tile_shape, part],
        unit,
        where,
        back,
        probe,
        probe_peer,
        crop0,
        prop,
    )
    pgot = lax.ppermute(psend, "mode", near)
    got0 = lax.ppermute(send0, "mode", near)
    sums = [keep0 + got0, keep1 + got1]
    totals = [s[0] + lax.ppermute(s[1], "mode", far_away) for s in sums]
    pieces_in = lax.all_to_all(pkeep + pgot, "tile", 0, 0)
    mine = jnp.sum(pieces_in, axis=0)
    pieces_out = lax.all_to_all(jnp.broadcast_to(mine[None], block), "tile", 0, 0)
    probe_grad = jnp.transpose(pieces_out, (1, 2, 0, 3, 4)).reshape(probe.shape)

    total = jnp.stack(totals, axis=1)
    up = [(i, i + 1) for i in range(tiles - 1)]
    down = [(j, i) for i, j in up]
    before = lax.ppermute(total[..., -MARGIN:], "tile", up)
    after = lax.ppermute(total[..., :MARGIN], "tile", down)
    pad = [(0, 0)] * 3
    grads = (
        total
        + jnp.pad(before, pad + [(0, size - MARGIN)])
        + jnp.pad(after, pad + [(size - MARGIN, 0)])
    )
    return (grads[0][None], grads[1][None], probe_grad)


def solution(mesh):
    placed = (
        P("tile", None, "mode", None),
        P("tile", None, "mode", None),
        P(None, "mode", None, None),
        P("tile", None, None, None),
        P("tile", None, None),
    )
    return jax.shard_map(
        body,
        mesh=mesh,
        in_specs=placed,
        out_specs=(
            P("tile", None, "mode", None),
            P("tile", None, "mode", None),
            P(None, "mode", None, None),
        ),
        check_vma=False,
    )
```
